32 devices in a mesh: dp: 16 (over z, y, x), group: 2 (over core).
Axes of the slice: x: 2, y: 2, z: 4, core: 2. Of those that a mesh axis runs over, the one named last changes fastest.
Arguments:
- acts_first: bfloat16 [32, 32, 32, 256], P(('dp', 'group'))
- grads_first: bfloat16 [32, 32, 32, 256], P(('dp', 'group'))
- acts_second: bfloat16 [32, 32, 32, 256], P(('dp', 'group'))
- grads_second: bfloat16 [32, 16, 16, 256], P(('dp', 'group'))
- grad_w: bfloat16 [2, 256, 2304], P(None, 'dp'), may hold values from -6 to 6
- owner: int32 [2], replicated, may hold values from 0 to 7, as said below
- basis_in: bfloat16 [8, 256, 256], P('group'), may hold values from -0.375 to 0.375
- basis_spatial: bfloat16 [8, 9, 9], P('group'), may hold values from -2 to 2
- basis_out: bfloat16 [8, 256, 256], P('group'), may hold values from -0.375 to 0.375
Outputs:
- precond: bfloat16 [2, 256, 2304], P(None, 'dp')
- factor_in: float32 [2, 256, 256], replicated
- factor_spatial: float32 [2, 9, 9], replicated
- factor_out: float32 [2, 256, 256], replicated
The draws below stay inside these ranges and needn't reach their ends.
Inputs may be any that keep to these rules, and one draw needn't show every extreme that they name: owner[l] is the slot that holds layer l's bases, one of the 4 slots of group owner[l] // 4; no two layers share a slot.
All inputs are finite; a program needn't handle non-finite values.
Results may differ from the reference program's by a relative error of at most 0.0045.
Values may be sent and summed in bfloat16 or wider, within the bound.
A program may use at most 64 MiB of HBM per device.

```python
import math
import jax
import jax.numpy as jnp
from jax import lax

C = 256
HI = 32
LAYERS = 2
SLOTS = 4
HO = 16
IMAGES = 32
GROUPS = 2


def scaled_field(key, side_len):
    noise_key, chan_key, image_key = jax.random.split(key, 3)
    field_shape = (IMAGES, side_len, side_len, C)
    noise_vals = jax.random.normal(noise_key, field_shape, jnp.float32)
    chan_scale = jnp.exp(jax.random.uniform(chan_key, (C,), jnp.float32, math.log(0.3), math.log(3.0)))
    image_ramp = jnp.arange(IMAGES, dtype=jnp.float32) / IMAGES
    image_scale = jnp.exp(math.log(0.6) + math.log(3.0) * image_ramp + jax.random.uniform(image_key, (IMAGES,), jnp.float32, -0.2, 0.2))
    return noise_vals * chan_scale * image_scale[:, None, None, None]


def draw_acts_first(key, part):
    return scaled_field(jax.random.fold_in(key, 11), HI).astype(jnp.bfloat16)


def draw_grads_first(key, part):
    return scaled_field(jax.random.fold_in(key, 12), HI).astype(jnp.bfloat16)


def draw_acts_second(key, part):
    return scaled_field(jax.random.fold_in(key, 13), HI).astype(jnp.bfloat16)


def draw_grads_second(key, part):
    return scaled_field(jax.random.fold_in(key, 14), HO).astype(jnp.bfloat16)


def draw_owner(key, part):
    lead_key, order_key = jax.random.split(jax.random.fold_in(key, 21))
    slot_total = GROUPS * SLOTS
    shuffled = jax.random.permutation(order_key, slot_total - 1)[:LAYERS]
    lead = jax.random.randint(lead_key, (), 0, LAYERS)
    slots = jnp.where(jnp.arange(LAYERS) == lead, slot_total - 1, shuffled)
    return slots.astype(jnp.int32)


def block_scale(stream_key, shape, cuts, smallest, high):
    gain, own = 1.0, jax.random.fold_in(stream_key, 6)
    for position, blocks in cuts:
        draws = jnp.exp(jax.random.uniform(jax.random.fold_in(own, position), (blocks,), jnp.float32, smallest / len(cuts), high / len(cuts)))
        gain = gain * jnp.repeat(draws, shape[position] // blocks).reshape([-1 if axis == position else 1 for axis in range(len(shape))])
    return gain


def bell_draw(stream_key, shape, spread, bound, pieces=(), kind=jnp.bfloat16):
    gain = block_scale(stream_key, shape, pieces, -0.22, 0.18) if pieces else 1.0
    values = jax.random.normal(stream_key, shape, jnp.float32) * spread * gain
    return jnp.minimum(jnp.maximum(values, -bound), bound).astype(kind)


def setup_inputs(seed: int = 0) -> dict:
    splits = jax.random.split(jax.random.key(seed), 10)
    return {
        "acts_first": draw_acts_first(jax.random.fold_in(splits[9], 71), 0),
        "grads_first": draw_grads_first(jax.random.fold_in(splits[9], 71), 0),
        "acts_second": draw_acts_second(jax.random.fold_in(splits[9], 71), 0),
        "grads_second": draw_grads_second(jax.random.fold_in(splits[9], 71), 0),
        "grad_w": bell_draw(splits[4], (LAYERS, C, 9 * C), 1.0, 6.0, ((1, 16),)),
        "owner": draw_owner(jax.random.fold_in(splits[9], 71), 0),
        "basis_in": bell_draw(splits[6], (GROUPS * SLOTS, C, C), C ** -0.5, 0.375, ((0, 2),)),
        "basis_spatial": bell_draw(splits[7], (GROUPS * SLOTS, 9, 9), 9 ** -0.5, 2.0, ((0, 2),)),
        "basis_out": bell_draw(splits[8], (GROUPS * SLOTS, C, C), C ** -0.5, 0.375, ((0, 2),)),
    }


DAMPING = 0.1

def window_views(images, stride, out_side):
    padded = jnp.pad(images, ((0, 0), (1, 1), (1, 1), (0, 0)))
    extent = stride * (out_side - 1) + 1
    limit_n = images.shape[0]
    channels = images.shape[3]
    windows = []
    for row_off in range(3):
        for col_off in range(3):
            windows.append(lax.slice(padded, (0, row_off, col_off, 0), (limit_n, row_off + extent, col_off + extent, channels), (1, stride, stride, 1)))
    return jnp.stack(windows)

def gram_terms(images, grads_out, stride):
    stacked = window_views(images, stride, grads_out.shape[1])
    channels = images.shape[3]
    patch_rows = stacked.reshape(-1, channels)
    channel_sum = lax.dot_general(patch_rows, patch_rows, (((0,), (0,)), ((), ())), preferred_element_type=jnp.float32)
    tap_rows = stacked.reshape(9, -1)
    spatial_sum = lax.dot_general(tap_rows, tap_rows, (((1,), (1,)), ((), ())), preferred_element_type=jnp.float32)
    out_rows = grads_out.reshape(-1, channels)
    output_sum = lax.dot_general(out_rows, out_rows, (((0,), (0,)), ((), ())), preferred_element_type=jnp.float32)
    return (channel_sum, spatial_sum, output_sum)

def whole_factors(images, grads_out, stride):
    block_count = images.shape[0] // 16
    image_blocks = images.reshape((block_count, 16) + images.shape[1:])
    grad_blocks = grads_out.reshape((block_count, 16) + grads_out.shape[1:])
    channels = images.shape[3]

    def add_block(carry, pair_in):
        terms = gram_terms(pair_in[0], pair_in[1], stride)
        return ((carry[0] + terms[0], carry[1] + terms[1], carry[2] + terms[2]), None)
    start_sums = (jnp.zeros((channels, channels), jnp.float32), jnp.zeros((9, 9), jnp.float32), jnp.zeros((channels, channels), jnp.float32))
    totals, unused = lax.scan(add_block, start_sums, (image_blocks, grad_blocks))
    positions = images.shape[0] * grads_out.shape[1] * grads_out.shape[2]
    return (totals[0] / (9.0 * positions), totals[1] / (1.0 * channels * positions), totals[2] / (1.0 * positions))

def eigen_values(basis, factor):
    basis_f = basis.astype(jnp.float32)
    return lax.optimization_barrier(jnp.sum(basis_f * jnp.dot(factor, basis_f, precision=lax.Precision.HIGHEST), axis=0))

def rotated_grad(weights, basis_chan, basis_tap):
    outs_n, taps_n, chans_n = weights.shape
    inner_in = jnp.dot(weights.reshape(outs_n * taps_n, chans_n), basis_chan, preferred_element_type=jnp.float32).reshape(outs_n, taps_n, -1)
    turned = jnp.einsum('okj,kl->olj', inner_in, basis_tap.astype(jnp.float32), precision=lax.Precision.HIGHEST)
    return turned.astype(jnp.bfloat16)

def scaled_coords(rotated, basis_outc, scale_out, scale_tap, scale_in):
    chans_out = basis_outc.shape[0]
    projected = lax.dot_general(basis_outc, rotated.reshape(chans_out, -1), (((0,), (0,)), ((), ())), preferred_element_type=jnp.float32).reshape(rotated.shape)
    divisor = scale_out[:, None, None] * scale_tap[None, :, None] * scale_in[None, None, :] + DAMPING
    return (projected / divisor).astype(jnp.bfloat16)

def back_rows(coords, rows_basis, basis_chan, basis_tap):
    row_n = rows_basis.shape[0]
    col_n = coords.shape[2]
    turned_back = jnp.dot(rows_basis, coords.reshape(coords.shape[0], -1), preferred_element_type=jnp.float32).astype(jnp.bfloat16)
    chan_back = lax.dot_general(turned_back.reshape(row_n * 9, col_n), basis_chan, (((1,), (1,)), ((), ())), preferred_element_type=jnp.float32).reshape(row_n, 9, -1)
    return jnp.einsum('okc,lk->olc', chan_back, basis_tap.astype(jnp.float32), precision=lax.Precision.HIGHEST)

def reference(acts_first, grads_first, acts_second, grads_second, grad_w, owner, basis_in, basis_spatial, basis_out):
    layer_inputs = ((acts_first, grads_first, 1), (acts_second, grads_second, 2))
    precond_list, fin_list, fsp_list, fout_list = ([], [], [], [])
    for layer_idx in range(LAYERS):
        images, grads_out, stride = layer_inputs[layer_idx]
        channel_f, spatial_f, output_f = whole_factors(images, grads_out, stride)
        slot_index = owner[layer_idx].astype(jnp.int32)
        basis_chan = lax.dynamic_index_in_dim(basis_in, slot_index, 0, keepdims=False)
        basis_tap = lax.dynamic_index_in_dim(basis_spatial, slot_index, 0, keepdims=False)
        basis_outc = lax.dynamic_index_in_dim(basis_out, slot_index, 0, keepdims=False)
        scale_in = eigen_values(basis_chan, channel_f)
        scale_tap = eigen_values(basis_tap, spatial_f)
        scale_out = eigen_values(basis_outc, output_f)
        weights = grad_w[layer_idx].reshape(C, 9, C)
        rotated = rotated_grad(weights, basis_chan, basis_tap)
        coords = scaled_coords(rotated, basis_outc, scale_out, scale_tap, scale_in)
        result = back_rows(coords, basis_outc, basis_chan, basis_tap).astype(jnp.bfloat16).reshape(C, 9 * C)
        precond_list.append(result)
        fin_list.append(channel_f)
        fsp_list.append(spatial_f)
        fout_list.append(output_f)
    return (jnp.stack(precond_list), jnp.stack(fin_list), jnp.stack(fsp_list), jnp.stack(fout_list))
```

```python
import functools

import jax
import jax.numpy as jnp
from jax import lax
from jax.experimental import pallas as pl
from jax.experimental.pallas import tpu as pltpu
from jax.sharding import PartitionSpec as P

LAYERS = 2
DAMPING = 0.1
LANES = 128
MESH = pl.DeviceIdType.MESH
F32 = jnp.float32
BF16 = jnp.bfloat16
HIGH = lax.Precision.HIGHEST
CONTRACT_ROWS = (((0,), (0,)), ((), ()))
CONTRACT_COLS = (((1,), (1,)), ((), ()))


def dot_rows(a, b, precision=None):
    return lax.dot_general(a, b, CONTRACT_ROWS, precision=precision, preferred_element_type=F32)


def dot_cols(a, b):
    return lax.dot_general(a, b, CONTRACT_COLS, preferred_element_type=F32)


def tap_count(idx, stride, out_side):
    total = jnp.zeros(idx.shape, jnp.int32)
    for off in range(3):
        base = idx + 1 - off
        hit = (base >= 0) & (base <= stride * (out_side - 1)) & (base % stride == 0)
        total = total + hit.astype(jnp.int32)
    return total


def channel_gram(x, side, stride, out_side):
    pos = lax.broadcasted_iota(jnp.int32, x.shape, 0)
    count = tap_count(pos // side, stride, out_side) * tap_count(pos % side, stride, out_side)
    total = None
    for digit in (1, 2, 4, 8):
        if digit > (9 if stride == 1 else 4):
            continue
        if stride == 1 and digit == 1:
            part = jnp.where((count & 1) != 0, x, jnp.zeros_like(x))
        else:
            part = jnp.where((count & digit) != 0, x * digit, jnp.zeros_like(x))
        term = dot_rows(part, x)
        total = term if total is None else total + term
    return total


def spatial_gram(xp_ref, v_ref, side, stride, out_side):
    total = None
    for i in range(out_side):
        rows = xp_ref[stride * i * side:(stride * i + 3) * side, :]
        term = dot_cols(rows, rows)
        total = term if total is None else total + term
    span = 3 * side
    left = lax.broadcasted_iota(jnp.int32, (span, span), 0) % side
    right = lax.broadcasted_iota(jnp.int32, (span, span), 1) % side
    v_ref[...] = jnp.zeros(v_ref.shape, F32)
    lane_in = lax.broadcasted_iota(jnp.int32, (LANES, LANES), 0)
    lane_out = lax.broadcasted_iota(jnp.int32, (LANES, LANES), 1)
    result = None
    for b2 in range(3):
        for b1 in range(3):
            base = left + 1 - b1
            mask = (right - left == b2 - b1) & (base >= 0) & (base <= stride * (out_side - 1))
            mask = mask & (base % stride == 0)
            kept = jnp.where(mask, total, 0.0)
            for a in range(3):
                t = 3 * a + b1
                v_ref[b2, t:t + 1, 0:span] = jnp.sum(
                    kept[a * side:(a + 1) * side], axis=0, keepdims=True)
        pick = ((lane_in < span) & (lane_out == 3 * (lane_in // side) + b2)).astype(F32)
        term = jnp.dot(v_ref[b2], pick, precision=HIGH, preferred_element_type=F32)
        result = term if result is None else result + term
    return result


def mixed_taps(parts, coef):
    out = []
    for t in range(9):
        total = parts[0] * coef(0, t)
        for u in range(1, 9):
            total = total + parts[u] * coef(u, t)
        out.append(total)
    return out


def through_basis(parts, basis, rows, flip):
    def product(a):
        if flip:
            return dot_cols(a, basis)
        return jnp.dot(a, basis, preferred_element_type=F32)
    if rows % 16 == 0:
        whole = product(jnp.concatenate(parts, axis=0))
        return [whole[u * rows:(u + 1) * rows] for u in range(9)]
    return [product(part) for part in parts]


def local_kernel(dims, info_ref, qs_ref, x0_ref, g0_ref, x1_ref, g1_ref, w_ref, qa_ref,
                 gram_ref, rot_ref, xp_ref, v_ref):
    side, outs, strides, images, chans, rows, dp = dims
    for l, (x_ref, g_ref) in enumerate(((x0_ref, g0_ref), (x1_ref, g1_ref))):
        base = l * 2 * chans
        fin = fsp = None
        xp_ref[0:side, :] = jnp.zeros((side, chans), BF16)
        xp_ref[side * (side + 1):side * (side + 2), :] = jnp.zeros((side, chans), BF16)
        for n in range(images):
            x = x_ref[n * side * side:(n + 1) * side * side, :]
            xp_ref[side:side * (side + 1), :] = x
            part = channel_gram(x, side, strides[l], outs[l])
            fin = part if fin is None else fin + part
            part = spatial_gram(xp_ref, v_ref, side, strides[l], outs[l])
            fsp = part if fsp is None else fsp + part
        g = g_ref[...]
        gram_ref[base:base + chans, :] = fin.astype(BF16)
        half = chans // 2
        gram_ref[base + half:base + half + 16, 0:LANES] = fsp.astype(BF16)
        gram_ref[base + chans:base + 2 * chans, :] = dot_rows(g, g).astype(BF16)
    per = 9 * chans // LANES
    for k in range(LAYERS * per, rot_ref.shape[0] * rot_ref.shape[1]):
        rot_ref[k % dp, k // dp] = jnp.zeros((rows, LANES), BF16)
    for l in range(LAYERS):
        basis = qa_ref[info_ref[l]]
        parts = [w_ref[l, :, u * chans:(u + 1) * chans] for u in range(9)]
        inner = through_basis(parts, basis, rows, False)
        turned = mixed_taps(inner, lambda u, t: qs_ref[l, 9 * u + t])
        for c in range(per):
            k = l * per + c
            lane = (c * LANES) % chans
            rot_ref[k % dp, k // dp] = turned[c * LANES // chans][:, lane:lane + LANES].astype(BF16)


def remote(src, dst, send, recv, axis, peer):
    return pltpu.make_async_remote_copy(src_ref=src, dst_ref=dst, send_sem=send, recv_sem=recv,
                                        device_id={axis: peer}, device_id_type=MESH)


def enter(dp, ng, me, grp):
    barrier = pltpu.get_barrier_semaphore()

    def greet(k, c):
        pl.semaphore_signal(barrier, inc=1, device_id={"dp": lax.rem(me + k, dp)},
                            device_id_type=MESH)
        return c
    lax.fori_loop(1, dp, greet, 0)
    for q in range(1, ng):
        pl.semaphore_signal(barrier, inc=1, device_id={"group": lax.rem(grp + q, ng)},
                            device_id_type=MESH)
    pl.semaphore_wait(barrier, dp + ng - 2)


def each(n, fn):
    def body(k, c):
        fn(k)
        return c
    lax.fori_loop(1, n, body, 0)


def share_kernel(dp, ng, gram_ref, rot_ref, full_ref, rotin_ref, ga_ref, h_ref, hb_ref,
                 sa, ra, sb, rb, sc, rc, sd, rd, st, rt, lt):
    me, grp = lax.axis_index("dp"), lax.axis_index("group")
    enter(dp, ng, me, grp)

    def copy_a(q):
        to = lax.rem(grp + q, ng)
        return remote(gram_ref.at[to], ga_ref.at[q - 1], sa.at[q], ra.at[q], "group", to)

    def copy_t(k):
        to = lax.rem(me + k, dp)
        return remote(rot_ref.at[to], rotin_ref.at[:, me], st.at[k], rt.at[k], "dp", to)

    def copy_b(k):
        to = lax.rem(me + k, dp)
        return remote(h_ref.at[to], hb_ref.at[k - 1], sb.at[k], rb.at[k], "dp", to)

    def copy_c(k):
        to = lax.rem(me + k, dp)
        return remote(full_ref.at[grp, me], full_ref.at[grp, me], sc.at[k], rc.at[k], "dp", to)

    def copy_d(k, q):
        to = lax.rem(grp + q, ng)
        block = full_ref.at[grp, lax.rem(me + dp - k, dp)]
        return remote(block, block, sd.at[q, k], rd.at[q, k], "group", to)

    own = pltpu.make_async_copy(rot_ref.at[me], rotin_ref.at[:, me], lt)
    for q in range(1, ng):
        copy_a(q).start()
    own.start()
    each(dp, lambda k: copy_t(k).start())
    for q in range(1, ng):
        copy_a(q).wait_recv()
    total = gram_ref[grp].astype(F32)
    for q in range(1, ng):
        total = total + ga_ref[q - 1].astype(F32)
    h_ref[...] = total.astype(BF16)
    each(dp, lambda k: copy_b(k).start())
    each(dp, lambda k: copy_b(k).wait_recv())
    total = h_ref[me].astype(F32)
    total = lax.fori_loop(0, dp - 1, lambda k, t: t + hb_ref[k].astype(F32), total)
    full_ref[grp, me] = total.astype(BF16)
    each(dp, lambda k: copy_c(k).start())
    for q in range(1, ng):
        copy_d(0, q).start()

    def pass_on(k):
        copy_c(k).wait_recv()
        for q in range(1, ng):
            copy_d(k, q).start()
    each(dp, pass_on)
    for q in range(1, ng):
        copy_d(0, q).wait()
    for q in range(1, ng):
        copy_a(q).wait_send()

    def finish(k):
        copy_b(k).wait_send()
        copy_c(k).wait_send()
        copy_t(k).wait()
        for q in range(1, ng):
            copy_d(k, q).wait()
    each(dp, finish)
    own.wait()


def coords_kernel(dims, info_ref, gram_ref, rot_ref, qa_ref, qg_ref, qs_ref,
                  back_ref, fin_ref, fsp_ref, fout_ref, lin_ref, ltap_ref, lout_ref):
    chans, dp, slots, positions = dims
    half = chans // 2
    for l in range(LAYERS):
        base = l * 2 * chans
        fin = gram_ref[base:base + chans, :]
        corner = jnp.transpose(fin[0:half, half:chans].astype(F32))
        low = jnp.concatenate([corner, fin[half:chans, half:chans].astype(F32)], axis=1)
        fin = jnp.concatenate([fin[0:half].astype(F32), low], axis=0)
        fsp = gram_ref[base + half:base + half + 16, 0:LANES].astype(F32)
        fout = gram_ref[base + chans:base + 2 * chans, :]
        fsp = fsp / (1.0 * chans * positions[l])
        fin_ref[l] = fin / (9.0 * positions[l])
        fout_ref[l] = fout.astype(F32) / (1.0 * positions[l])
        fsp_ref[l] = fsp[0:9, 0:9]
        qa, qg, qs = qa_ref[info_ref[l]], qg_ref[info_ref[l]], qs_ref[l]
        prod = jnp.dot(fin.astype(BF16), qa, preferred_element_type=F32)
        lin_ref[l] = jnp.sum(qa.astype(F32) * prod, axis=0, keepdims=True) / (9.0 * positions[l])
        prod = qg.astype(F32) * jnp.dot(fout, qg, preferred_element_type=F32)
        lout_ref[l] = dot_rows(prod / (1.0 * positions[l]), jnp.ones((chans, LANES), F32), HIGH)
        turned = fsp[:, 0:1] * qs[0:1, :]
        for v in range(1, 9):
            turned = turned + fsp[:, v:v + 1] * qs[v:v + 1, :]
        ltap_ref[l] = jnp.sum(turned * qs, axis=0, keepdims=True)
    per = 9 * chans // LANES
    split = chans // LANES
    for s in range(slots):
        k = jnp.minimum(s * dp + info_ref[4], LAYERS * per - 1)
        l = k // per
        c = k % per
        lane = lax.broadcasted_iota(jnp.int32, (1, LANES), 1)
        tap = jnp.sum(jnp.where(lane == c // split, ltap_ref[l], 0.0), axis=1, keepdims=True)
        row = lin_ref[l]
        scale_in = row[:, 0:LANES]
        for piece in range(1, split):
            scale_in = jnp.where(c % split == piece, row[:, piece * LANES:(piece + 1) * LANES],
                                 scale_in)
        qg = qg_ref[info_ref[l]]
        projected = dot_rows(qg, rot_ref[s])
        divisor = (lout_ref[l] * tap) * scale_in + DAMPING
        coords = (projected / divisor).astype(BF16)
        back_ref[s] = jnp.dot(qg, coords, preferred_element_type=F32).astype(BF16)


def rows_kernel(dims, info_ref, qs_ref, back_ref, qa_ref, out_ref, in_ref, own_ref, peer_ref,
                st, rt, lt, sx, rx):
    dp, ng, rows, chans = dims
    me, grp = lax.axis_index("dp"), lax.axis_index("group")
    enter(dp, ng, me, grp)

    def copy_t(k):
        to = lax.rem(me + k, dp)
        return remote(back_ref.at[:, to], in_ref.at[me], st.at[k], rt.at[k], "dp", to)

    def copy_x(q):
        return remote(own_ref, peer_ref.at[q - 1], sx.at[q], rx.at[q], "group",
                      lax.rem(grp + q, ng))

    own = pltpu.make_async_copy(back_ref.at[:, me], in_ref.at[me], lt)
    own.start()
    each(dp, lambda k: copy_t(k).start())
    own.wait()
    each(dp, lambda k: copy_t(k).wait())
    per = 9 * chans // LANES
    split = chans // LANES
    for l in range(LAYERS):
        basis = qa_ref[info_ref[l]]
        mine = info_ref[2 + l] == 1
        parts = []
        for t in range(9):
            pieces = []
            for piece in range(split):
                k = l * per + t * split + piece
                pieces.append(in_ref[k % dp, k // dp])
            parts.append(jnp.concatenate(pieces, axis=1))
        chan = through_basis(parts, basis, rows, True)
        turned = mixed_taps(chan, lambda t, u: qs_ref[l, 9 * u + t])
        for u in range(9):
            value = jnp.where(mine, turned[u], jnp.zeros_like(turned[u]))
            own_ref[l, :, u * chans:(u + 1) * chans] = value.astype(BF16)
    for q in range(1, ng):
        copy_x(q).start()
    for q in range(1, ng):
        copy_x(q).wait()
    total = own_ref[...]
    for q in range(1, ng):
        total = total + peer_ref[q - 1]
    out_ref[...] = total


def on_device(dp, ng, acts_first, grads_first, acts_second, grads_second, grad_w, owner,
              basis_in, basis_spatial, basis_out):
    images, side = acts_first.shape[0], acts_first.shape[1]
    chans = basis_in.shape[1]
    rows = grad_w.shape[1]
    slot_total = basis_in.shape[0]
    outs = (grads_first.shape[1], grads_second.shape[1])
    positions = tuple(images * o * o * dp * ng for o in outs)
    slots = -(-LAYERS * 9 * chans // LANES // dp)
    gram_rows = 2 * LAYERS * chans
    slice_rows = gram_rows // (dp * ng)
    vmem = pl.BlockSpec(memory_space=pltpu.VMEM)
    smem = pl.BlockSpec(memory_space=pltpu.SMEM)
    struct = jax.ShapeDtypeStruct
    dma = pltpu.SemaphoreType.DMA

    local = owner % slot_total
    holds = (owner // slot_total == lax.axis_index("group")).astype(jnp.int32)
    info = jnp.concatenate([local, holds, lax.axis_index("dp").astype(jnp.int32)[None]])
    taps = jnp.stack([lax.dynamic_index_in_dim(basis_spatial, local[l], 0, keepdims=False)
                      for l in range(LAYERS)]).astype(F32)
    taps_flat = taps.reshape(LAYERS, 81)
    taps_wide = jnp.pad(taps, ((0, 0), (0, 7), (0, LANES - 9)))

    gram, rot = pl.pallas_call(
        functools.partial(local_kernel, (side, outs, (1, 2), images, chans, rows, dp)),
        out_shape=(struct((gram_rows, chans), BF16), struct((dp, slots, rows, LANES), BF16)),
        in_specs=[smem, smem] + [vmem] * 6,
        out_specs=(vmem, vmem),
        scratch_shapes=[pltpu.VMEM(((side + 2) * side, chans), BF16),
                        pltpu.VMEM((3, 16, LANES), F32)],
        compiler_params=pltpu.CompilerParams(vmem_limit_bytes=40 << 20),
        name="local_terms",
    )(info, taps_flat, acts_first.reshape(-1, chans), grads_first.reshape(-1, chans),
      acts_second.reshape(-1, chans), grads_second.reshape(-1, chans), grad_w, basis_in)

    full, rotin = pl.pallas_call(
        functools.partial(share_kernel, dp, ng),
        out_shape=(struct((ng, dp, slice_rows, chans), BF16),
                   struct((slots, dp, rows, LANES), BF16)),
        in_specs=[vmem, vmem],
        out_specs=(vmem, vmem),
        scratch_shapes=[pltpu.VMEM((ng - 1, dp, slice_rows, chans), BF16),
                        pltpu.VMEM((dp, slice_rows, chans), BF16),
                        pltpu.VMEM((dp - 1, slice_rows, chans), BF16),
                        dma((ng,)), dma((ng,)), dma((dp,)), dma((dp,)), dma((dp,)), dma((dp,)),
                        dma((ng, dp)), dma((ng, dp)), dma((dp,)), dma((dp,)), dma],
        compiler_params=pltpu.CompilerParams(collective_id=0, has_side_effects=True,
                                             vmem_limit_bytes=32 << 20),
        name="share_sums",
    )(gram.reshape(ng, dp, slice_rows, chans), rot)

    back, fin, fsp, fout = pl.pallas_call(
        functools.partial(coords_kernel, (chans, dp, slots, positions)),
        out_shape=(struct((slots, chans, LANES), BF16), struct((LAYERS, chans, chans), F32),
                   struct((LAYERS, 9, 9), F32), struct((LAYERS, chans, chans), F32)),
        in_specs=[smem] + [vmem] * 5,
        out_specs=(vmem,) * 4,
        scratch_shapes=[pltpu.VMEM((LAYERS, 1, chans), F32), pltpu.VMEM((LAYERS, 1, LANES), F32),
                        pltpu.VMEM((LAYERS, chans, LANES), F32)],
        compiler_params=pltpu.CompilerParams(vmem_limit_bytes=32 << 20),
        name="scaled_coords",
    )(info, full.reshape(gram_rows, chans), rotin.reshape(slots, chans, LANES),
      basis_in, basis_out, taps_wide)

    precond = pl.pallas_call(
        functools.partial(rows_kernel, (dp, ng, rows, chans)),
        out_shape=struct((LAYERS, rows, 9 * chans), BF16),
        in_specs=[smem, smem, vmem, vmem],
        out_specs=vmem,
        scratch_shapes=[pltpu.VMEM((dp, slots, rows, LANES), BF16),
                        pltpu.VMEM((LAYERS, rows, 9 * chans), BF16),
                        pltpu.VMEM((ng - 1, LAYERS, rows, 9 * chans), BF16),
                        dma((dp,)), dma((dp,)), dma, dma((ng,)), dma((ng,))],
        compiler_params=pltpu.CompilerParams(collective_id=1, has_side_effects=True,
                                             vmem_limit_bytes=32 << 20),
        name="back_rows",
    )(info, taps_flat, back.reshape(slots, dp, rows, LANES), basis_in)
    return precond, fin, fsp, fout


def solution(mesh):
    placed = (
        P(("dp", "group"), None, None, None),
        P(("dp", "group"), None, None, None),
        P(("dp", "group"), None, None, None),
        P(("dp", "group"), None, None, None),
        P(None, "dp", None),
        P(),
        P("group", None, None),
        P("group", None, None),
        P("group", None, None),
    )
    return jax.shard_map(
        functools.partial(on_device, mesh.shape["dp"], mesh.shape["group"]),
        mesh=mesh,
        in_specs=placed,
        out_specs=(P(None, "dp", None), P(), P(), P()),
        check_vma=False,
    )
```

```python
import functools

import jax
import jax.numpy as jnp
from jax import lax
from jax.experimental import pallas as pl
from jax.experimental.pallas import tpu as pltpu
from jax.sharding import PartitionSpec as P

LAYERS = 2
DAMPING = 0.1
LANES = 128
MESH = pl.DeviceIdType.MESH
F32 = jnp.float32
BF16 = jnp.bfloat16
HIGH = lax.Precision.HIGHEST
CONTRACT_ROWS = (((0,), (0,)), ((), ()))
CONTRACT_COLS = (((1,), (1,)), ((), ()))


def dot_rows(a, b, precision=None):
    return lax.dot_general(a, b, CONTRACT_ROWS, precision=precision, preferred_element_type=F32)


def dot_cols(a, b):
    return lax.dot_general(a, b, CONTRACT_COLS, preferred_element_type=F32)


def tap_count(idx, stride, out_side):
    total = jnp.zeros(idx.shape, jnp.int32)
    for off in range(3):
        base = idx + 1 - off
        hit = (base >= 0) & (base <= stride * (out_side - 1)) & (base % stride == 0)
        total = total + hit.astype(jnp.int32)
    return total


def channel_gram(x, side, stride, out_side):
    pos = lax.broadcasted_iota(jnp.int32, x.shape, 0)
    count = tap_count(pos // side, stride, out_side) * tap_count(pos % side, stride, out_side)
    total = None
    for digit in (1, 2, 4, 8):
        if digit > (9 if stride == 1 else 4):
            continue
        if stride == 1 and digit == 1:
            part = jnp.where((count & 1) != 0, x, jnp.zeros_like(x))
        else:
            part = jnp.where((count & digit) != 0, x * digit, jnp.zeros_like(x))
        term = dot_rows(part, x)
        total = term if total is None else total + term
    return total


def spatial_gram(xp_ref, v_ref, side, stride, out_side):
    total = None
    for i in range(out_side):
        rows = xp_ref[stride * i * side:(stride * i + 3) * side, :]
        term = dot_cols(rows, rows)
        total = term if total is None else total + term
    span = 3 * side
    left = lax.broadcasted_iota(jnp.int32, (span, span), 0) % side
    right = lax.broadcasted_iota(jnp.int32, (span, span), 1) % side
    v_ref[...] = jnp.zeros(v_ref.shape, F32)
    lane_in = lax.broadcasted_iota(jnp.int32, (LANES, LANES), 0)
    lane_out = lax.broadcasted_iota(jnp.int32, (LANES, LANES), 1)
    result = None
    for b2 in range(3):
        for b1 in range(3):
            base = left + 1 - b1
            mask = (right - left == b2 - b1) & (base >= 0) & (base <= stride * (out_side - 1))
            mask = mask & (base % stride == 0)
            kept = jnp.where(mask, total, 0.0)
            for a in range(3):
                t = 3 * a + b1
                v_ref[b2, t:t + 1, 0:span] = jnp.sum(
                    kept[a * side:(a + 1) * side], axis=0, keepdims=True)
        pick = ((lane_in < span) & (lane_out == 3 * (lane_in // side) + b2)).astype(F32)
        term = jnp.dot(v_ref[b2], pick, precision=HIGH, preferred_element_type=F32)
        result = term if result is None else result + term
    return result


def mixed_taps(parts, coef):
    out = []
    for t in range(9):
        total = parts[0] * coef(0, t)
        for u in range(1, 9):
            total = total + parts[u] * coef(u, t)
        out.append(total)
    return out


def through_basis(parts, basis, rows, flip):
    def product(a):
        if flip:
            return dot_cols(a, basis)
        return jnp.dot(a, basis, preferred_element_type=F32)
    if rows % 16 == 0:
        whole = product(jnp.concatenate(parts, axis=0))
        return [whole[u * rows:(u + 1) * rows] for u in range(9)]
    return [product(part) for part in parts]


def put_rows(ref, dp, start, value):
    size = ref.shape[2]
    step = min(size, value.shape[0])
    for j in range(0, value.shape[0], step):
        i, off = divmod(start + j, size)
        piece = value[j:j + step].astype(BF16)
        ref[i // dp, i % dp, off:off + step, 0:value.shape[1]] = piece


def local_loads(pairs, sems):
    loads = {}
    for i, (src, dst) in enumerate(pairs):
        step = dst.shape[0] // 4 if dst.shape[0] % 4 == 0 else dst.shape[0] // 2
        loads[i] = [pltpu.make_async_copy(src.at[pl.ds(j * step, step)],
                                          dst.at[pl.ds(j * step, step)], sems.at[i, j])
                    for j in range(dst.shape[0] // step)]
    for i in range(len(pairs)):
        for load in loads[i]:
            load.start()

    def arrive(i):
        for load in loads[i]:
            load.wait()
    return arrive


def local_grams(dims, arrive, x0_ref, g0_ref, x1_ref, g1_ref, gram_ref, xp_ref, v_ref):
    side, outs, strides, images, chans, rows, dp, slot_total = dims
    for l, (x_ref, g_ref) in enumerate(((x0_ref, g0_ref), (x1_ref, g1_ref))):
        base = l * 2 * chans
        fin = fsp = None
        arrive(2 * l)
        xp_ref[0:side, :] = jnp.zeros((side, chans), BF16)
        xp_ref[side * (side + 1):side * (side + 2), :] = jnp.zeros((side, chans), BF16)
        for n in range(images):
            x = x_ref[n * side * side:(n + 1) * side * side, :]
            xp_ref[side:side * (side + 1), :] = x
            part = channel_gram(x, side, strides[l], outs[l])
            fin = part if fin is None else fin + part
            part = spatial_gram(xp_ref, v_ref, side, strides[l], outs[l])
            fsp = part if fsp is None else fsp + part
        arrive(2 * l + 1)
        g = g_ref[...]
        put_rows(gram_ref, dp, base, fin)
        half = chans // 2
        put_rows(gram_ref, dp, base + half, fsp)
        put_rows(gram_ref, dp, base + chans, dot_rows(g, g))


def local_rotation(dims, owner_ref, qs_ref, w_ref, qa_ref, rot_ref):
    side, outs, strides, images, chans, rows, dp, slot_total = dims
    slots = [owner_ref[l] % slot_total for l in range(LAYERS)]
    per = 9 * chans // LANES
    for k in range(LAYERS * per, rot_ref.shape[0] * rot_ref.shape[1]):
        rot_ref[k % dp, k // dp] = jnp.zeros((rows, LANES), BF16)
    for l in range(LAYERS):
        basis = qa_ref[slots[l]]
        parts = [w_ref[l, :, u * chans:(u + 1) * chans] for u in range(9)]
        inner = through_basis(parts, basis, rows, False)
        turned = mixed_taps(inner, lambda u, t: qs_ref[slots[l], 9 * u + t])
        for c in range(per):
            k = l * per + c
            lane = (c * LANES) % chans
            rot_ref[k % dp, k // dp] = turned[c * LANES // chans][:, lane:lane + LANES].astype(BF16)


def remote(src, dst, send, recv, axis, peer):
    return pltpu.make_async_remote_copy(src_ref=src, dst_ref=dst, send_sem=send, recv_sem=recv,
                                        device_id={axis: peer}, device_id_type=MESH)


def greet_all(dp, ng, me, grp):
    barrier = pltpu.get_barrier_semaphore()

    def greet(k, c):
        pl.semaphore_signal(barrier, inc=1, device_id={"dp": lax.rem(me + k, dp)},
                            device_id_type=MESH)
        return c
    lax.fori_loop(1, dp, greet, 0)
    for q in range(1, ng):
        pl.semaphore_signal(barrier, inc=1, device_id={"group": lax.rem(grp + q, ng)},
                            device_id_type=MESH)


def all_here(dp, ng):
    pl.semaphore_wait(pltpu.get_barrier_semaphore(), dp + ng - 2)


def enter(dp, ng, me, grp):
    greet_all(dp, ng, me, grp)
    all_here(dp, ng)


def each(n, fn):
    def body(k, c):
        fn(k)
        return c
    lax.fori_loop(1, n, body, 0)


def share_kernel(dims, ng, owner_ref, qs_ref, x0_hbm, g0_hbm, x1_hbm, g1_hbm, w_hbm, qa_hbm,
                 full_ref, rotin_ref, gram_ref, rot_ref, x0_ref, g0_ref, x1_ref, g1_ref, w_ref,
                 qa_ref, xp_ref, v_ref, loads, ga_ref, h_ref, hb_ref,
                 sa, ra, sb, rb, sc, rc, sd, rd, st, rt, lt):
    dp = dims[6]
    me, grp = lax.axis_index("dp"), lax.axis_index("group")
    arrive = local_loads(((x0_hbm, x0_ref), (g0_hbm, g0_ref), (x1_hbm, x1_ref), (g1_hbm, g1_ref),
                          (w_hbm, w_ref), (qa_hbm, qa_ref)), loads)
    greet_all(dp, ng, me, grp)
    local_grams(dims, arrive, x0_ref, g0_ref, x1_ref, g1_ref, gram_ref, xp_ref, v_ref)
    all_here(dp, ng)

    def copy_a(q):
        to = lax.rem(grp + q, ng)
        return remote(gram_ref.at[to], ga_ref.at[q - 1], sa.at[q], ra.at[q], "group", to)

    def copy_t(k):
        to = lax.rem(me + k, dp)
        return remote(rot_ref.at[to], rotin_ref.at[:, me], st.at[k], rt.at[k], "dp", to)

    def copy_b(k):
        to = lax.rem(me + k, dp)
        return remote(h_ref.at[to], hb_ref.at[k - 1], sb.at[k], rb.at[k], "dp", to)

    def copy_c(k):
        to = lax.rem(me + k, dp)
        return remote(full_ref.at[grp, me], full_ref.at[grp, me], sc.at[k], rc.at[k], "dp", to)

    def copy_d(k, q):
        to = lax.rem(grp + q, ng)
        block = full_ref.at[grp, lax.rem(me + dp - k, dp)]
        return remote(block, block, sd.at[q, k], rd.at[q, k], "group", to)

    own = pltpu.make_async_copy(rot_ref.at[me], rotin_ref.at[:, me], lt)
    for q in range(1, ng):
        copy_a(q).start()
    arrive(4)
    arrive(5)
    local_rotation(dims, owner_ref, qs_ref, w_ref, qa_ref, rot_ref)
    own.start()
    each(dp, lambda k: copy_t(k).start())
    for q in range(1, ng):
        copy_a(q).wait_recv()
    total = gram_ref[grp].astype(F32)
    for q in range(1, ng):
        total = total + ga_ref[q - 1].astype(F32)
    h_ref[...] = total.astype(BF16)
    each(dp, lambda k: copy_b(k).start())
    each(dp, lambda k: copy_b(k).wait_recv())
    total = h_ref[me].astype(F32)
    total = lax.fori_loop(0, dp - 1, lambda k, t: t + hb_ref[k].astype(F32), total)
    full_ref[grp, me] = total.astype(BF16)
    each(dp, lambda k: copy_c(k).start())
    for q in range(1, ng):
        copy_d(0, q).start()

    def pass_on(k):
        copy_c(k).wait_recv()
        for q in range(1, ng):
            copy_d(k, q).start()
    each(dp, pass_on)
    for q in range(1, ng):
        copy_d(0, q).wait()
    for q in range(1, ng):
        copy_a(q).wait_send()

    def finish(k):
        copy_b(k).wait_send()
        copy_c(k).wait_send()
        copy_t(k).wait()
        for q in range(1, ng):
            copy_d(k, q).wait()
    each(dp, finish)
    own.wait()


def coords_kernel(dims, owner_ref, gram_ref, rot_ref, qa_ref, qg_ref, qs_ref,
                  back_ref, fin_ref, fsp_ref, fout_ref, lin_ref, ltap_ref, lout_ref):
    chans, dp, slots, positions, slot_total = dims
    me = lax.axis_index("dp")
    half = chans // 2
    for l in range(LAYERS):
        base = l * 2 * chans
        fin = gram_ref[base:base + chans, :]
        corner = jnp.transpose(fin[0:half, half:chans].astype(F32))
        low = jnp.concatenate([corner, fin[half:chans, half:chans].astype(F32)], axis=1)
        fin = jnp.concatenate([fin[0:half].astype(F32), low], axis=0)
        fsp = gram_ref[base + half:base + half + 16, 0:LANES].astype(F32)
        fout = gram_ref[base + chans:base + 2 * chans, :]
        fsp = fsp / (1.0 * chans * positions[l])
        fin_ref[l] = fin / (9.0 * positions[l])
        fout_ref[l] = fout.astype(F32) / (1.0 * positions[l])
        fsp_ref[l] = fsp[0:9, 0:9]
        slot = owner_ref[l] % slot_total
        qa, qg, qs = qa_ref[slot], qg_ref[slot], qs_ref[slot]
        prod = jnp.dot(fin.astype(BF16), qa, preferred_element_type=F32)
        lin_ref[l] = jnp.sum(qa.astype(F32) * prod, axis=0, keepdims=True) / (9.0 * positions[l])
        prod = qg.astype(F32) * jnp.dot(fout, qg, preferred_element_type=F32)
        lout_ref[l] = dot_rows(prod / (1.0 * positions[l]), jnp.ones((chans, LANES), F32), HIGH)
        turned = fsp[:, 0:1] * qs[0:1, :]
        for v in range(1, 9):
            turned = turned + fsp[:, v:v + 1] * qs[v:v + 1, :]
        ltap_ref[l] = jnp.sum(turned * qs, axis=0, keepdims=True)
    per = 9 * chans // LANES
    split = chans // LANES
    for s in range(slots):
        k = jnp.minimum(s * dp + me, LAYERS * per - 1)
        l = k // per
        c = k % per
        lane = lax.broadcasted_iota(jnp.int32, (1, LANES), 1)
        tap = jnp.sum(jnp.where(lane == c // split, ltap_ref[l], 0.0), axis=1, keepdims=True)
        row = lin_ref[l]
        scale_in = row[:, 0:LANES]
        for piece in range(1, split):
            scale_in = jnp.where(c % split == piece, row[:, piece * LANES:(piece + 1) * LANES],
                                 scale_in)
        qg = qg_ref[owner_ref[l] % slot_total]
        projected = dot_rows(qg, rot_ref[s])
        divisor = (lout_ref[l] * tap) * scale_in + DAMPING
        coords = (projected / divisor).astype(BF16)
        back_ref[s] = jnp.dot(qg, coords, preferred_element_type=F32).astype(BF16)


def rows_kernel(dims, owner_ref, qs_ref, back_ref, qa_ref, out_ref, in_ref, own_ref, peer_ref,
                st, rt, lt, sx, rx):
    dp, ng, rows, chans, slot_total = dims
    me, grp = lax.axis_index("dp"), lax.axis_index("group")
    enter(dp, ng, me, grp)

    def copy_t(k):
        to = lax.rem(me + k, dp)
        return remote(back_ref.at[:, to], in_ref.at[me], st.at[k], rt.at[k], "dp", to)

    def copy_x(q):
        return remote(own_ref, peer_ref.at[q - 1], sx.at[q], rx.at[q], "group",
                      lax.rem(grp + q, ng))

    own = pltpu.make_async_copy(back_ref.at[:, me], in_ref.at[me], lt)
    own.start()
    each(dp, lambda k: copy_t(k).start())
    own.wait()
    each(dp, lambda k: copy_t(k).wait())
    per = 9 * chans // LANES
    split = chans // LANES
    for l in range(LAYERS):
        slot = owner_ref[l] % slot_total
        basis = qa_ref[slot]
        mine = owner_ref[l] // slot_total == grp
        parts = []
        for t in range(9):
            pieces = []
            for piece in range(split):
                k = l * per + t * split + piece
                pieces.append(in_ref[k % dp, k // dp])
            parts.append(jnp.concatenate(pieces, axis=1))
        chan = through_basis(parts, basis, rows, True)
        turned = mixed_taps(chan, lambda t, u: qs_ref[slot, 9 * u + t])
        for u in range(9):
            value = jnp.where(mine, turned[u], jnp.zeros_like(turned[u]))
            own_ref[l, :, u * chans:(u + 1) * chans] = value.astype(BF16)
    for q in range(1, ng):
        copy_x(q).start()
    for q in range(1, ng):
        copy_x(q).wait()
    total = own_ref[...]
    for q in range(1, ng):
        total = total + peer_ref[q - 1]
    out_ref[...] = total


def on_device(dp, ng, acts_first, grads_first, acts_second, grads_second, grad_w, owner,
              basis_in, basis_spatial, basis_out):
    images, side = acts_first.shape[0], acts_first.shape[1]
    chans = basis_in.shape[1]
    rows = grad_w.shape[1]
    slot_total = basis_in.shape[0]
    outs = (grads_first.shape[1], grads_second.shape[1])
    positions = tuple(images * o * o * dp * ng for o in outs)
    slots = -(-LAYERS * 9 * chans // LANES // dp)
    gram_rows = 2 * LAYERS * chans
    slice_rows = gram_rows // (dp * ng)
    vmem = pl.BlockSpec(memory_space=pltpu.VMEM)
    smem = pl.BlockSpec(memory_space=pltpu.SMEM)
    struct = jax.ShapeDtypeStruct
    dma = pltpu.SemaphoreType.DMA

    taps = basis_spatial.astype(F32)
    taps_flat = taps.reshape(slot_total, 81)
    taps_wide = jnp.pad(taps, ((0, 0), (0, 7), (0, LANES - 9)))
    hbm = pl.BlockSpec(memory_space=pltpu.HBM)

    full, rotin = pl.pallas_call(
        functools.partial(share_kernel, (side, outs, (1, 2), images, chans, rows, dp, slot_total),
                          ng),
        out_shape=(struct((ng, dp, slice_rows, chans), BF16),
                   struct((slots, dp, rows, LANES), BF16)),
        in_specs=[smem, smem] + [hbm] * 6,
        out_specs=(vmem, vmem),
        scratch_shapes=[pltpu.VMEM((ng, dp, slice_rows, chans), BF16),
                        pltpu.VMEM((dp, slots, rows, LANES), BF16),
                        pltpu.VMEM((images * side * side, chans), BF16),
                        pltpu.VMEM((images * outs[0] * outs[0], chans), BF16),
                        pltpu.VMEM((images * side * side, chans), BF16),
                        pltpu.VMEM((images * outs[1] * outs[1], chans), BF16),
                        pltpu.VMEM(grad_w.shape, BF16),
                        pltpu.VMEM(basis_in.shape, BF16),
                        pltpu.VMEM(((side + 2) * side, chans), BF16),
                        pltpu.VMEM((3, 16, LANES), F32), dma((6, 4)),
                        pltpu.VMEM((ng - 1, dp, slice_rows, chans), BF16),
                        pltpu.VMEM((dp, slice_rows, chans), BF16),
                        pltpu.VMEM((dp - 1, slice_rows, chans), BF16),
                        dma((ng,)), dma((ng,)), dma((dp,)), dma((dp,)), dma((dp,)), dma((dp,)),
                        dma((ng, dp)), dma((ng, dp)), dma((dp,)), dma((dp,)), dma],
        compiler_params=pltpu.CompilerParams(collective_id=0, has_side_effects=True,
                                             vmem_limit_bytes=62 << 20),
        name="share_sums",
    )(owner, taps_flat, acts_first.reshape(-1, chans), grads_first.reshape(-1, chans),
      acts_second.reshape(-1, chans), grads_second.reshape(-1, chans), grad_w, basis_in)

    back, fin, fsp, fout = pl.pallas_call(
        functools.partial(coords_kernel, (chans, dp, slots, positions, slot_total)),
        out_shape=(struct((slots, chans, LANES), BF16), struct((LAYERS, chans, chans), F32),
                   struct((LAYERS, 9, 9), F32), struct((LAYERS, chans, chans), F32)),
        in_specs=[smem] + [vmem] * 5,
        out_specs=(vmem,) * 4,
        scratch_shapes=[pltpu.VMEM((LAYERS, 1, chans), F32), pltpu.VMEM((LAYERS, 1, LANES), F32),
                        pltpu.VMEM((LAYERS, chans, LANES), F32)],
        compiler_params=pltpu.CompilerParams(vmem_limit_bytes=32 << 20),
        name="scaled_coords",
    )(owner, full.reshape(gram_rows, chans), rotin.reshape(slots, chans, LANES),
      basis_in, basis_out, taps_wide)

    precond = pl.pallas_call(
        functools.partial(rows_kernel, (dp, ng, rows, chans, slot_total)),
        out_shape=struct((LAYERS, rows, 9 * chans), BF16),
        in_specs=[smem, smem, vmem, vmem],
        out_specs=vmem,
        scratch_shapes=[pltpu.VMEM((dp, slots, rows, LANES), BF16),
                        pltpu.VMEM((LAYERS, rows, 9 * chans), BF16),
                        pltpu.VMEM((ng - 1, LAYERS, rows, 9 * chans), BF16),
                        dma((dp,)), dma((dp,)), dma, dma((ng,)), dma((ng,))],
        compiler_params=pltpu.CompilerParams(collective_id=1, has_side_effects=True,
                                             vmem_limit_bytes=32 << 20),
        name="back_rows",
    )(owner, taps_flat, back.reshape(slots, dp, rows, LANES), basis_in)
    return precond, fin, fsp, fout


def solution(mesh):
    placed = (
        P(("dp", "group"), None, None, None),
        P(("dp", "group"), None, None, None),
        P(("dp", "group"), None, None, None),
        P(("dp", "group"), None, None, None),
        P(None, "dp", None),
        P(),
        P("group", None, None),
        P("group", None, None),
        P("group", None, None),
    )
    return jax.shard_map(
        functools.partial(on_device, mesh.shape["dp"], mesh.shape["group"]),
        mesh=mesh,
        in_specs=placed,
        out_specs=(P(None, "dp", None), P(), P(), P()),
        check_vma=False,
    )
```

```python
import functools

import jax
import jax.numpy as jnp
from jax import lax
from jax.experimental import pallas as pl
from jax.experimental.pallas import tpu as pltpu
from jax.sharding import PartitionSpec as P

LAYERS = 2
DAMPING = 0.1
LANES = 128
MESH = pl.DeviceIdType.MESH
F32 = jnp.float32
BF16 = jnp.bfloat16
HIGH = lax.Precision.HIGHEST
CONTRACT_ROWS = (((0,), (0,)), ((), ()))
CONTRACT_COLS = (((1,), (1,)), ((), ()))


def dot_rows(a, b, precision=None):
    return lax.dot_general(a, b, CONTRACT_ROWS, precision=precision, preferred_element_type=F32)


def dot_cols(a, b):
    return lax.dot_general(a, b, CONTRACT_COLS, preferred_element_type=F32)


def tap_count(idx, stride, out_side):
    total = jnp.zeros(idx.shape, jnp.int32)
    for off in range(3):
        base = idx + 1 - off
        hit = (base >= 0) & (base <= stride * (out_side - 1)) & (base % stride == 0)
        total = total + hit.astype(jnp.int32)
    return total


def channel_gram(x, side, stride, out_side):
    pos = lax.broadcasted_iota(jnp.int32, x.shape, 0)
    count = tap_count(pos // side, stride, out_side) * tap_count(pos % side, stride, out_side)
    total = None
    for digit in (1, 2, 4, 8):
        if digit > (9 if stride == 1 else 4):
            continue
        if stride == 1 and digit == 1:
            part = jnp.where((count & 1) != 0, x, jnp.zeros_like(x))
        else:
            part = jnp.where((count & digit) != 0, x * digit, jnp.zeros_like(x))
        term = dot_rows(part, x)
        total = term if total is None else total + term
    return total


def spatial_gram(xp_ref, v_ref, side, stride, out_side):
    total = None
    for i in range(out_side):
        rows = xp_ref[stride * i * side:(stride * i + 3) * side, :]
        term = dot_cols(rows, rows)
        total = term if total is None else total + term
    span = 3 * side
    left = lax.broadcasted_iota(jnp.int32, (span, span), 0) % side
    right = lax.broadcasted_iota(jnp.int32, (span, span), 1) % side
    v_ref[...] = jnp.zeros(v_ref.shape, F32)
    lane_in = lax.broadcasted_iota(jnp.int32, (LANES, LANES), 0)
    lane_out = lax.broadcasted_iota(jnp.int32, (LANES, LANES), 1)
    result = None
    for b2 in range(3):
        for b1 in range(3):
            base = left + 1 - b1
            mask = (right - left == b2 - b1) & (base >= 0) & (base <= stride * (out_side - 1))
            mask = mask & (base % stride == 0)
            kept = jnp.where(mask, total, 0.0)
            for a in range(3):
                t = 3 * a + b1
                v_ref[b2, t:t + 1, 0:span] = jnp.sum(
                    kept[a * side:(a + 1) * side], axis=0, keepdims=True)
        pick = ((lane_in < span) & (lane_out == 3 * (lane_in // side) + b2)).astype(F32)
        term = jnp.dot(v_ref[b2], pick, precision=HIGH, preferred_element_type=F32)
        result = term if result is None else result + term
    return result


def mixed_taps(parts, coef):
    out = []
    for t in range(9):
        total = parts[0] * coef(0, t)
        for u in range(1, 9):
            total = total + parts[u] * coef(u, t)
        out.append(total)
    return out


def through_basis(parts, basis, rows, flip):
    def product(a):
        if flip:
            return dot_cols(a, basis)
        return jnp.dot(a, basis, preferred_element_type=F32)
    if rows % 16 == 0:
        whole = product(jnp.concatenate(parts, axis=0))
        return [whole[u * rows:(u + 1) * rows] for u in range(9)]
    return [product(part) for part in parts]


def put_rows(ref, dp, start, value):
    size = ref.shape[2]
    step = min(size, value.shape[0])
    for j in range(0, value.shape[0], step):
        i, off = divmod(start + j, size)
        piece = value[j:j + step].astype(BF16)
        ref[i // dp, i % dp, off:off + step, 0:value.shape[1]] = piece


def stacked(pieces):
    if pieces[0].shape[0] % 16 == 0:
        return jnp.concatenate(pieces, axis=0)
    return jnp.concatenate([piece.astype(F32) for piece in pieces], axis=0).astype(BF16)


def take_rows(ref, dp, start, count):
    size = ref.shape[2]
    first = start // size
    return stacked([ref[i // dp, i % dp] for i in range(first, first + count // size)])


def local_loads(pairs, sems):
    loads = {}
    for i, (src, dst) in enumerate(pairs):
        step = dst.shape[0] // 4 if dst.shape[0] % 4 == 0 else dst.shape[0] // 2
        loads[i] = [pltpu.make_async_copy(src.at[pl.ds(j * step, step)],
                                          dst.at[pl.ds(j * step, step)], sems.at[i, j])
                    for j in range(dst.shape[0] // step)]
    for i in range(len(pairs)):
        for load in loads[i]:
            load.start()

    def arrive(i):
        for load in loads[i]:
            load.wait()
    return arrive


def local_grams(dims, arrive, x0_ref, g0_ref, x1_ref, g1_ref, gram_ref, xp_ref, v_ref):
    side, outs, strides, images, chans, rows, dp, slot_total = dims
    for l, (x_ref, g_ref) in enumerate(((x0_ref, g0_ref), (x1_ref, g1_ref))):
        base = l * 2 * chans
        fin = fsp = None
        arrive(2 * l)
        xp_ref[0:side, :] = jnp.zeros((side, chans), BF16)
        xp_ref[side * (side + 1):side * (side + 2), :] = jnp.zeros((side, chans), BF16)
        for n in range(images):
            x = x_ref[n * side * side:(n + 1) * side * side, :]
            xp_ref[side:side * (side + 1), :] = x
            part = channel_gram(x, side, strides[l], outs[l])
            fin = part if fin is None else fin + part
            part = spatial_gram(xp_ref, v_ref, side, strides[l], outs[l])
            fsp = part if fsp is None else fsp + part
        arrive(2 * l + 1)
        g = g_ref[...]
        put_rows(gram_ref, dp, base, fin)
        half = chans // 2
        put_rows(gram_ref, dp, base + half, fsp)
        put_rows(gram_ref, dp, base + chans, dot_rows(g, g))


def local_rotation(dims, owner_ref, qs_ref, w_ref, qa_ref, rot_ref):
    side, outs, strides, images, chans, rows, dp, slot_total = dims
    slots = [owner_ref[l] % slot_total for l in range(LAYERS)]
    per = 9 * chans // LANES
    for k in range(LAYERS * per, rot_ref.shape[0] * rot_ref.shape[1]):
        rot_ref[k % dp, k // dp] = jnp.zeros((rows, LANES), BF16)
    for l in range(LAYERS):
        basis = qa_ref[slots[l]]
        parts = [w_ref[l, :, u * chans:(u + 1) * chans] for u in range(9)]
        inner = through_basis(parts, basis, rows, False)
        turned = mixed_taps(inner, lambda u, t: qs_ref[slots[l], 9 * u + t])
        for c in range(per):
            k = l * per + c
            lane = (c * LANES) % chans
            rot_ref[k % dp, k // dp] = turned[c * LANES // chans][:, lane:lane + LANES].astype(BF16)


def remote(src, dst, send, recv, axis, peer):
    return pltpu.make_async_remote_copy(src_ref=src, dst_ref=dst, send_sem=send, recv_sem=recv,
                                        device_id={axis: peer}, device_id_type=MESH)


def greet_all(dp, ng, me, grp):
    barrier = pltpu.get_barrier_semaphore()

    def greet(k, c):
        pl.semaphore_signal(barrier, inc=1, device_id={"dp": lax.rem(me + k, dp)},
                            device_id_type=MESH)
        return c
    lax.fori_loop(1, dp, greet, 0)
    for q in range(1, ng):
        pl.semaphore_signal(barrier, inc=1, device_id={"group": lax.rem(grp + q, ng)},
                            device_id_type=MESH)


def all_here(dp, ng):
    pl.semaphore_wait(pltpu.get_barrier_semaphore(), dp + ng - 2)


def each(n, fn):
    def body(k, c):
        fn(k)
        return c
    lax.fori_loop(1, n, body, 0)


def share(dims, ng, owner_ref, qs_ref, x0_hbm, g0_hbm, x1_hbm, g1_hbm, w_hbm, qa_hbm,
                 qg_hbm, full_ref, rotin_ref, qg_ref, gram_ref, rot_ref, x0_ref, g0_ref, x1_ref, g1_ref, w_ref,
                 qa_ref, xp_ref, v_ref, loads, ga_ref, h_ref, hb_ref,
                 sa, ra, sb, rb, sc, rc, sd, rd, st, rt, lt):
    dp = dims[6]
    me, grp = lax.axis_index("dp"), lax.axis_index("group")
    arrive = local_loads(((x0_hbm, x0_ref), (g0_hbm, g0_ref), (x1_hbm, x1_ref), (g1_hbm, g1_ref),
                          (w_hbm, w_ref), (qa_hbm, qa_ref), (qg_hbm, qg_ref)), loads)
    greet_all(dp, ng, me, grp)
    local_grams(dims, arrive, x0_ref, g0_ref, x1_ref, g1_ref, gram_ref, xp_ref, v_ref)
    all_here(dp, ng)

    def copy_a(q):
        to = lax.rem(grp + q, ng)
        return remote(gram_ref.at[to], ga_ref.at[q - 1], sa.at[q], ra.at[q], "group", to)

    def copy_t(k):
        to = lax.rem(me + k, dp)
        return remote(rot_ref.at[to], rotin_ref.at[:, me], st.at[k], rt.at[k], "dp", to)

    def copy_b(k):
        to = lax.rem(me + k, dp)
        return remote(h_ref.at[to], hb_ref.at[k - 1], sb.at[k], rb.at[k], "dp", to)

    def copy_c(k):
        to = lax.rem(me + k, dp)
        return remote(full_ref.at[grp, me], full_ref.at[grp, me], sc.at[k], rc.at[k], "dp", to)

    def copy_d(k, q):
        to = lax.rem(grp + q, ng)
        block = full_ref.at[grp, lax.rem(me + dp - k, dp)]
        return remote(block, block, sd.at[q, k], rd.at[q, k], "group", to)

    own = pltpu.make_async_copy(rot_ref.at[me], rotin_ref.at[:, me], lt)
    for q in range(1, ng):
        copy_a(q).start()
    arrive(4)
    arrive(5)
    local_rotation(dims, owner_ref, qs_ref, w_ref, qa_ref, rot_ref)
    own.start()
    each(dp, lambda k: copy_t(k).start())
    for q in range(1, ng):
        copy_a(q).wait_recv()
    total = gram_ref[grp].astype(F32)
    for q in range(1, ng):
        total = total + ga_ref[q - 1].astype(F32)
    h_ref[...] = total.astype(BF16)
    each(dp, lambda k: copy_b(k).start())
    each(dp, lambda k: copy_b(k).wait_recv())
    total = h_ref[me].astype(F32)
    total = lax.fori_loop(0, dp - 1, lambda k, t: t + hb_ref[k].astype(F32), total)
    full_ref[grp, me] = total.astype(BF16)
    each(dp, lambda k: copy_c(k).start())
    for q in range(1, ng):
        copy_d(0, q).start()

    def pass_on(k):
        copy_c(k).wait_recv()
        for q in range(1, ng):
            copy_d(k, q).start()
    each(dp, pass_on)
    for q in range(1, ng):
        copy_d(0, q).wait()
    for q in range(1, ng):
        copy_a(q).wait_send()

    def finish(k):
        copy_b(k).wait_send()
        copy_c(k).wait_send()
        copy_t(k).wait()
        for q in range(1, ng):
            copy_d(k, q).wait()
    each(dp, finish)
    own.wait()
    arrive(6)


def coords_step(dims, owner_ref, gram_ref, rot_ref, qa_ref, qg_ref, qs_ref,
                  back_ref, fin_ref, fsp_ref, fout_ref, lin_ref, ltap_ref, lout_ref):
    chans, dp, slots, positions, slot_total = dims
    me = lax.axis_index("dp")
    half = chans // 2
    for l in range(LAYERS):
        base = l * 2 * chans
        fin = take_rows(gram_ref, dp, base, chans)
        fsp = fin[half:half + 16, 0:LANES].astype(F32)
        corner = jnp.transpose(fin[0:half, half:chans].astype(F32))
        low = jnp.concatenate([corner, fin[half:chans, half:chans].astype(F32)], axis=1)
        fin = jnp.concatenate([fin[0:half].astype(F32), low], axis=0)
        fout = take_rows(gram_ref, dp, base + chans, chans)
        fsp = fsp / (1.0 * chans * positions[l])
        fin_ref[l] = fin / (9.0 * positions[l])
        fout_ref[l] = fout.astype(F32) / (1.0 * positions[l])
        fsp_ref[l] = fsp[0:9, 0:9]
        slot = owner_ref[l] % slot_total
        qa, qg, qs = qa_ref[slot], qg_ref[slot], qs_ref[slot]
        prod = jnp.dot(fin.astype(BF16), qa, preferred_element_type=F32)
        lin_ref[l] = jnp.sum(qa.astype(F32) * prod, axis=0, keepdims=True) / (9.0 * positions[l])
        prod = qg.astype(F32) * jnp.dot(fout, qg, preferred_element_type=F32)
        lout_ref[l] = dot_rows(prod / (1.0 * positions[l]), jnp.ones((chans, LANES), F32), HIGH)
        turned = fsp[:, 0:1] * qs[0:1, :]
        for v in range(1, 9):
            turned = turned + fsp[:, v:v + 1] * qs[v:v + 1, :]
        ltap_ref[l] = jnp.sum(turned * qs, axis=0, keepdims=True)
    per = 9 * chans // LANES
    split = chans // LANES
    for s in range(slots):
        k = jnp.minimum(s * dp + me, LAYERS * per - 1)
        l = k // per
        c = k % per
        lane = lax.broadcasted_iota(jnp.int32, (1, LANES), 1)
        tap = jnp.sum(jnp.where(lane == c // split, ltap_ref[l], 0.0), axis=1, keepdims=True)
        row = lin_ref[l]
        scale_in = row[:, 0:LANES]
        for piece in range(1, split):
            scale_in = jnp.where(c % split == piece, row[:, piece * LANES:(piece + 1) * LANES],
                                 scale_in)
        qg = qg_ref[owner_ref[l] % slot_total]
        projected = dot_rows(qg, stacked([rot_ref[s, e] for e in range(dp)]))
        divisor = (lout_ref[l] * tap) * scale_in + DAMPING
        coords = (projected / divisor).astype(BF16)
        back = jnp.dot(qg, coords, preferred_element_type=F32)
        rows = back_ref.shape[2]
        for e in range(dp):
            back_ref[s, e] = back[e * rows:(e + 1) * rows].astype(BF16)


def rows_step(dims, owner_ref, qs_ref, back_ref, qa_ref, out_ref, in_ref, own_ref, peer_ref,
                st, rt, lt, sx, rx):
    dp, ng, rows, chans, slot_total = dims
    me, grp = lax.axis_index("dp"), lax.axis_index("group")

    def copy_t(k):
        to = lax.rem(me + k, dp)
        return remote(back_ref.at[:, to], in_ref.at[me], st.at[k], rt.at[k], "dp", to)

    def copy_x(q):
        return remote(own_ref, peer_ref.at[q - 1], sx.at[q], rx.at[q], "group",
                      lax.rem(grp + q, ng))

    own = pltpu.make_async_copy(back_ref.at[:, me], in_ref.at[me], lt)
    own.start()
    each(dp, lambda k: copy_t(k).start())
    own.wait()
    each(dp, lambda k: copy_t(k).wait())
    per = 9 * chans // LANES
    split = chans // LANES
    for l in range(LAYERS):
        slot = owner_ref[l] % slot_total
        basis = qa_ref[slot]
        mine = owner_ref[l] // slot_total == grp
        parts = []
        for t in range(9):
            pieces = []
            for piece in range(split):
                k = l * per + t * split + piece
                pieces.append(in_ref[k % dp, k // dp])
            parts.append(jnp.concatenate(pieces, axis=1))
        chan = through_basis(parts, basis, rows, True)
        turned = mixed_taps(chan, lambda t, u: qs_ref[slot, 9 * u + t])
        for u in range(9):
            value = jnp.where(mine, turned[u], jnp.zeros_like(turned[u]))
            own_ref[l, :, u * chans:(u + 1) * chans] = value.astype(BF16)
    for q in range(1, ng):
        copy_x(q).start()
    for q in range(1, ng):
        copy_x(q).wait()
    total = own_ref[...]
    for q in range(1, ng):
        total = total + peer_ref[q - 1]
    out_ref[...] = total


def whole_kernel(dims, ng, slots, positions, *refs):
    side, outs, strides, images, chans, rows, dp, slot_total = dims
    owner_ref, qs_ref = refs[0:2]
    sources = refs[2:9]
    wide_ref = refs[9]
    out_ref, fin_ref, fsp_ref, fout_ref = refs[10:14]
    full_ref, rotin_ref, qg_ref, back_ref = refs[14:18]
    lin_ref, ltap_ref, lout_ref = refs[18:21]
    row_scratch = refs[21:29]
    rest = refs[29:]
    qa_ref = rest[7]
    share(dims, ng, owner_ref, qs_ref, *sources, full_ref, rotin_ref, qg_ref, *rest)
    coords_step((chans, dp, slots, positions, slot_total), owner_ref, full_ref, rotin_ref, qa_ref,
                qg_ref, wide_ref, back_ref, fin_ref, fsp_ref, fout_ref, lin_ref, ltap_ref, lout_ref)
    rows_step((dp, ng, rows, chans, slot_total), owner_ref, qs_ref, back_ref, qa_ref, out_ref,
              *row_scratch)


def on_device(dp, ng, acts_first, grads_first, acts_second, grads_second, grad_w, owner,
              basis_in, basis_spatial, basis_out):
    images, side = acts_first.shape[0], acts_first.shape[1]
    chans = basis_in.shape[1]
    rows = grad_w.shape[1]
    slot_total = basis_in.shape[0]
    outs = (grads_first.shape[1], grads_second.shape[1])
    positions = tuple(images * o * o * dp * ng for o in outs)
    slots = -(-LAYERS * 9 * chans // LANES // dp)
    gram_rows = 2 * LAYERS * chans
    slice_rows = gram_rows // (dp * ng)
    vmem = pl.BlockSpec(memory_space=pltpu.VMEM)
    smem = pl.BlockSpec(memory_space=pltpu.SMEM)
    struct = jax.ShapeDtypeStruct
    dma = pltpu.SemaphoreType.DMA

    taps = basis_spatial.astype(F32)
    taps_flat = taps.reshape(slot_total, 81)
    taps_wide = jnp.pad(taps, ((0, 0), (0, 7), (0, LANES - 9)))
    hbm = pl.BlockSpec(memory_space=pltpu.HBM)

    dims = (side, outs, (1, 2), images, chans, rows, dp, slot_total)
    return pl.pallas_call(
        functools.partial(whole_kernel, dims, ng, slots, positions),
        out_shape=(struct((LAYERS, rows, 9 * chans), BF16), struct((LAYERS, chans, chans), F32),
                   struct((LAYERS, 9, 9), F32), struct((LAYERS, chans, chans), F32)),
        in_specs=[smem, smem] + [hbm] * 7 + [vmem],
        out_specs=(vmem,) * 4,
        scratch_shapes=[
            pltpu.VMEM((ng, dp, slice_rows, chans), BF16),
            pltpu.VMEM((slots, dp, rows, LANES), BF16),
            pltpu.VMEM(basis_out.shape, BF16),
            pltpu.VMEM((slots, dp, rows, LANES), BF16),
            pltpu.VMEM((LAYERS, 1, chans), F32),
            pltpu.VMEM((LAYERS, 1, LANES), F32),
            pltpu.VMEM((LAYERS, chans, LANES), F32),
            pltpu.VMEM((dp, slots, rows, LANES), BF16),
            pltpu.VMEM((LAYERS, rows, 9 * chans), BF16),
            pltpu.VMEM((ng - 1, LAYERS, rows, 9 * chans), BF16),
            dma((dp,)), dma((dp,)), dma, dma((ng,)), dma((ng,)),
            pltpu.VMEM((ng, dp, slice_rows, chans), BF16),
            pltpu.VMEM((dp, slots, rows, LANES), BF16),
            pltpu.VMEM((images * side * side, chans), BF16),
            pltpu.VMEM((images * outs[0] * outs[0], chans), BF16),
            pltpu.VMEM((images * side * side, chans), BF16),
            pltpu.VMEM((images * outs[1] * outs[1], chans), BF16),
            pltpu.VMEM(grad_w.shape, BF16),
            pltpu.VMEM(basis_in.shape, BF16),
            pltpu.VMEM(((side + 2) * side, chans), BF16),
            pltpu.VMEM((3, 16, LANES), F32),
            dma((7, 4)),
            pltpu.VMEM((ng - 1, dp, slice_rows, chans), BF16),
            pltpu.VMEM((dp, slice_rows, chans), BF16),
            pltpu.VMEM((dp - 1, slice_rows, chans), BF16),
            dma((ng,)), dma((ng,)), dma((dp,)), dma((dp,)), dma((dp,)), dma((dp,)),
            dma((ng, dp)), dma((ng, dp)), dma((dp,)), dma((dp,)), dma],
        compiler_params=pltpu.CompilerParams(collective_id=0, has_side_effects=True,
                                             vmem_limit_bytes=62 << 20),
        name="precondition",
    )(owner, taps_flat, acts_first.reshape(-1, chans), grads_first.reshape(-1, chans),
      acts_second.reshape(-1, chans), grads_second.reshape(-1, chans), grad_w, basis_in,
      basis_out, taps_wide)


def solution(mesh):
    placed = (
        P(("dp", "group"), None, None, None),
        P(("dp", "group"), None, None, None),
        P(("dp", "group"), None, None, None),
        P(("dp", "group"), None, None, None),
        P(None, "dp", None),
        P(),
        P("group", None, None),
        P("group", None, None),
        P("group", None, None),
    )
    return jax.shard_map(
        functools.partial(on_device, mesh.shape["dp"], mesh.shape["group"]),
        mesh=mesh,
        in_specs=placed,
        out_specs=(P(None, "dp", None), P(), P(), P()),
        check_vma=False,
    )
```
